32 devices in a mesh: row: 8 (over z, y), col: 4 (over x, core).
Axes of the slice: x: 2, y: 2, z: 4, core: 2. Of those that a mesh axis runs over, the one named last changes fastest.
Arguments:
- amplitudes: float32 [64, 2, 640], P('row', None, 'col'), may hold values from -6 to 6
- integrals: float32 [2, 640, 640, 640], P(None, 'col', 'row'), may hold values from -0.5 to 0.5
- virt_irrep: int32 [640], replicated, may hold values from 0 to 7
- pair_irrep: int32 [64], replicated, may hold values from 0 to 7
- tile_mask: int32 [8, 8], replicated, may hold values 0 or 1
Outputs:
- residual: float32 [64, 640, 640], P('col', 'row')
The draws below stay inside these ranges and needn't reach their ends.
All inputs are finite; a program needn't handle non-finite values.
Results may differ from the reference program's by a relative error of at most 0.000071.
Values sent between devices are 32-bit elements; how exact they have to be, the bound alone decides.
A program may use at most 192 MiB of HBM per device.

```python
import jax
import jax.numpy as jnp
from jax import lax

V = 640
NIRREP = 8
CS = 2
P_SIZE = 64


def touch_ends(array, key, least, high):
    index_at = [jax.random.randint(jax.random.fold_in(key, axis), (), 0, length) for axis, length in enumerate(array.shape)]
    longest = array.shape.index(max(array.shape))
    beside = index_at[:longest] + [(index_at[longest] + 1) % array.shape[longest]] + index_at[longest + 1:]
    return array.at[tuple(index_at)].set(least).at[tuple(beside)].set(high)


def level_of(stream_key, dims, shards, least, top_value):
    def one(dim, parts):
        steps = jax.random.uniform(jax.random.fold_in(jax.random.fold_in(stream_key, 6), dim), (parts,), jnp.float32, least / len(shards), top_value / len(shards))
        return jnp.repeat(jnp.exp(steps), dims[dim] // parts).reshape((-1,) + (1,) * (len(dims) - dim - 1))

    loudness = one(*shards[0])
    for cut in shards[1:]:
        loudness = loudness * one(*cut)
    return loudness


def noise(rng, shape, width, reach, split=(), kind=jnp.bfloat16):
    loudness = level_of(rng, shape, split, -0.22, 0.18) if split else 1.0
    array = jax.random.normal(rng, shape, jnp.float32) * width * loudness
    return jnp.minimum(jnp.maximum(array, -reach), reach).astype(kind)


def setup_inputs(seed: int = 0) -> dict:
    streams_of = jax.random.split(jax.random.key(seed), 6)
    return {
        "amplitudes": noise(streams_of[0], (P_SIZE, CS, V), 1.0, 6.0, ((0, 8), (2, 4)), jnp.float32),
        "integrals": noise(streams_of[1], (CS, V, V, V), (CS * V // 10) ** -0.5, 0.5, ((1, 4), (2, 8)), jnp.float32),
        "virt_irrep": touch_ends(jax.random.randint(streams_of[2], (V,), 0, NIRREP), jax.random.fold_in(streams_of[2], 1), 0, NIRREP - 1).astype(jnp.int32),
        "pair_irrep": touch_ends(jax.random.randint(streams_of[3], (P_SIZE,), 0, NIRREP), jax.random.fold_in(streams_of[3], 1), 0, NIRREP - 1).astype(jnp.int32),
        "tile_mask": touch_ends((jax.random.randint(streams_of[4], (NIRREP, NIRREP), 0, 4) < 3).astype(jnp.int32), jax.random.fold_in(streams_of[4], 1), 0, 1),
    }


def reference(amplitudes, integrals, virt_irrep, pair_irrep, tile_mask):
    c_labels = virt_irrep[:CS]
    screen = tile_mask.astype(amplitudes.dtype)[c_labels[:, None], virt_irrep[None, :]]
    allowed = jnp.bitwise_xor(c_labels[:, None], virt_irrep[None, :])[None, :, :] == pair_irrep[:, None, None]
    masked = amplitudes * screen[None, :, :] * allowed.astype(amplitudes.dtype)
    ladder = jnp.dot(masked.reshape(P_SIZE, CS * V), integrals.reshape(CS * V, V * V), precision=lax.Precision.HIGHEST, preferred_element_type=jnp.float32).reshape(P_SIZE, V, V)
    mirrored = ladder - jnp.transpose(ladder, (0, 2, 1))
    kept_mask = jnp.bitwise_xor(virt_irrep[:, None], virt_irrep[None, :])[None, :, :] == pair_irrep[:, None, None]
    return mirrored * kept_mask.astype(mirrored.dtype)
```

```python
import functools

import jax
import jax.numpy as jnp
from jax import lax
from jax.experimental import pallas as pl
from jax.experimental.pallas import tpu as pltpu
from jax.sharding import PartitionSpec as P

MESH = pl.DeviceIdType.MESH
F32 = jnp.float32
BF16 = jnp.bfloat16
I32 = jnp.int32


def split(x):
    high = x.astype(BF16)
    return high, (x - high.astype(F32)).astype(BF16)


def mm(a, b):
    return jnp.dot(a, b, preferred_element_type=F32)


def mm_nt(a, b):
    return lax.dot_general(a, b, (((1,), (1,)), ((), ())), preferred_element_type=F32)


def mm3(a, b):
    return jnp.dot(a, b, precision=lax.Precision.HIGHEST, preferred_element_type=F32)


def lanes_of(x, index):
    return jnp.take_along_axis(x, index, axis=1, mode="promise_in_bounds")


def exchange(blocks, axis):
    return lax.all_to_all(blocks, axis, split_axis=0, concat_axis=0, tiled=True)


def iota(shape, axis):
    return lax.broadcasted_iota(I32, shape, axis)


def one(x):
    return x.astype(F32).astype(BF16)


def plan_kernel(nrow, ncol, slab, d_width, nirr, cap, jcap, lanes, virt_ref, row_ref, fits_ref, perm_ref, loc_ref):
    width = row_ref.shape[1]
    aw = width // nrow
    col = lax.axis_index("col")
    labels = jnp.broadcast_to(row_ref[...], (nirr, width))
    onehot = one(labels == iota((nirr, width), 0))
    block, at = iota((lanes, width), 0), iota((lanes, width), 1)
    size = jnp.where(block < nrow, aw, jnp.where(block < nrow + ncol, d_width, width))
    first = jnp.where(block < nrow, block * aw, jnp.where(block < nrow + ncol, (block - nrow) * d_width, 0))
    member = (at >= first) & (at < first + size) & (block <= nrow + ncol)
    counts = mm_nt(onehot, one(member))
    lane = iota((nirr, lanes), 1)
    room = jnp.where(lane < nrow, cap, jnp.where(lane < nrow + ncol, jcap, lanes)).astype(F32)
    fits_ref[0] = 1 - jnp.max((counts > room).astype(I32))
    sel = one(iota((d_width, width), 1) == iota((d_width, width), 0) + col * d_width)
    local_labels = mm_nt(one(labels), sel).astype(I32)
    hit = (local_labels == iota((nirr, d_width), 0)).astype(F32)
    ahead = one(iota((d_width, d_width), 1) < iota((d_width, d_width), 0))
    rank = jnp.sum(hit * mm_nt(hit.astype(BF16), ahead), axis=0, keepdims=True).astype(I32)
    loc_ref[0:8, :] = jnp.broadcast_to(local_labels[0:1], (8, d_width))
    loc_ref[8:16, :] = jnp.broadcast_to(rank, (8, d_width))
    jth = one(rank == iota((jcap, d_width), 0))
    d = iota((lanes, d_width), 1)
    for c in range(slab):
        mine = (local_labels[0:1] ^ virt_ref[c]) == iota((lanes, d_width), 0)
        tens = mm_nt(jth, one(jnp.where(mine, d >> 4, 0)))
        ones = mm_nt(jth, one(jnp.where(mine, d & 15, 0)))
        perm_ref[c * jcap:(c + 1) * jcap, :] = (tens * 16.0 + ones).astype(I32) + c * d_width


def ladder_kernel(
    nrow, ncol, cap, jcap, nbuf, lag,
    virt_ref, pair_ref, keep_ref, perm_ref, row_ref, loc_ref, x_ref, w_ref,
    o_ref,
    wx_s, g_s, d_s, ft_s, e_s, r_s, lc_s, z_s, zr_s, zt_s, al_s, xb_s, idx_s, w_sem, gs_sem, gr_sem, es_sem, er_sem,
    zs_sem, zr_sem, *w_s,
):
    row, col = lax.axis_index("row"), lax.axis_index("col")
    depth, aw, width = w_ref.shape
    own_p, slab, d_width = x_ref.shape
    pairs = xb_s.shape[0]
    own = pairs // ncol
    chunks, rows_j, tile, _ = wx_s.shape
    steps = aw // tile
    lanes = ft_s.shape[0]
    nirr = keep_ref.shape[0]
    bits = nirr.bit_length() - 1
    hops = ncol.bit_length() - 1
    zw = idx_s.shape[2]

    def tile_of(t):
        return pl.ds(pl.multiple_of(t * tile, tile), tile)

    def w_copy(t, slot):
        return pltpu.make_async_copy(w_ref.at[:, tile_of(t), :], w_s[slot], w_sem.at[slot])

    for t in range(min(nbuf, steps)):
        w_copy(t, t).start()

    barrier = pltpu.get_barrier_semaphore()
    for off in range(1, nrow):
        pl.semaphore_signal(barrier, inc=1, device_id={"row": lax.rem(row + off, nrow)}, device_id_type=MESH)
    for k in range(hops):
        pl.semaphore_signal(barrier, inc=1, device_id={"col": col ^ (1 << k)}, device_id_type=MESH)
    pl.semaphore_wait(barrier, nrow - 1 + hops)

    mine = pl.ds(row * own_p, own_p)
    gathers = []
    for off in range(1, nrow):
        gathers.append(
            pltpu.make_async_remote_copy(
                src_ref=x_ref,
                dst_ref=g_s.at[mine],
                send_sem=gs_sem.at[off - 1],
                recv_sem=gr_sem.at[off - 1],
                device_id={"row": lax.rem(row + off, nrow)},
                device_id_type=MESH,
            )
        )
        gathers[-1].start()
    g_s[mine] = x_ref[...]

    labels = row_ref[...]
    for p in range(pairs):
        xb_s[p:p + 1, :] = labels ^ pair_ref[p]

    def label_rows(i, carry):
        for k in range(tile):
            al_s[pl.ds(i * tile + k, 1), :] = jnp.full((1, lanes), virt_ref[row * aw + i * tile + k], I32)
        return carry

    lax.fori_loop(0, steps, label_rows, 0)
    wide_labels = jnp.broadcast_to(labels, (nirr, width))
    hit = wide_labels == iota((nirr, width), 0)
    onehot = one(hit)
    ranks = []
    for v in range(chunks):
        ahead = one(iota((lanes, width), 1) < iota((lanes, width), 0) + v * lanes)
        ranks.append(mm_nt(onehot, ahead))
    rank = jnp.sum(hit.astype(F32) * jnp.concatenate(ranks, axis=1), axis=0, keepdims=True).astype(I32)
    ft_s[...] = one(iota((lanes, width), 0) == rank)
    before = one(iota((nrow, width), 1) < iota((nrow, width), 0) * aw)
    starts = mm_nt(before, one(jnp.broadcast_to(labels, (lanes, width)) == iota((lanes, width), 0))).astype(I32)
    sel = one(iota((lanes, width), 1) == iota((lanes, width), 0) + row * aw)
    own_labels = mm_nt(one(wide_labels), sel)
    own_hit = (own_labels == iota((nirr, lanes), 0).astype(F32)).astype(F32)
    own_ahead = one(iota((lanes, lanes), 1) < iota((lanes, lanes), 0))
    own_rank = jnp.sum(own_hit * mm_nt(own_hit.astype(BF16), own_ahead), axis=0, keepdims=True).astype(I32)
    slot_of = iota((lanes, lanes), 0)
    slot_of = jnp.where(slot_of < cap, slot_of, jnp.where(slot_of < 2 * cap, slot_of - cap, lanes))
    pick = (slot_of == own_rank).astype(F32).T[:aw, :2 * cap].astype(BF16)
    lane = iota((1, zw), 1)
    owner, pos = jnp.zeros((1, zw), I32), lane
    for p in range(own):
        owner = jnp.where(lane >= p * cap, pair_ref[col * own + p], owner)
        pos = jnp.where(lane >= p * cap, lane - p * cap, pos)

    def places(t, carry):
        al = al_s[tile_of(t), :]
        for s in range(nrow):
            begin = jnp.broadcast_to(starts[s:s + 1], (tile, lanes))
            for v in range(zw // lanes):
                at = slice(v * lanes, (v + 1) * lanes)
                index = lanes_of(begin, al ^ owner[:, at]) + pos[:, at]
                idx_s[s, tile_of(t), at] = jnp.minimum(index, lanes - 1)
        return carry

    lax.fori_loop(0, steps, places, 0)

    def spot(owner):
        return sum(((owner >> k) & 1) << (hops - 1 - k) for k in range(hops))

    def e_base(k):
        base = 0
        for b in range(k):
            base = base + ((col >> b) & 1) * (ncol >> (b + 1))
        return base

    def e_copy(t, k):
        half = ncol >> (k + 1)
        away = e_base(k) + (1 - ((col >> k) & 1)) * half
        return pltpu.make_async_remote_copy(
            src_ref=e_s.at[t, pl.ds(away, half)],
            dst_ref=r_s.at[t, pl.ds(ncol - 2 * half, half)],
            send_sem=es_sem.at[t, k],
            recv_sem=er_sem.at[t, k],
            device_id={"col": col ^ (1 << k)},
            device_id_type=MESH,
        )

    def z_copy(t, off):
        return pltpu.make_async_remote_copy(
            src_ref=z_s.at[off - 1, tile_of(t)],
            dst_ref=zr_s.at[row, tile_of(t)],
            send_sem=zs_sem.at[t, off - 1],
            recv_sem=zr_sem.at[t, off - 1],
            device_id={"row": lax.rem(row + off, nrow)},
            device_id_type=MESH,
        )

    for copy in gathers:
        copy.wait()

    lhs = jnp.zeros((pairs, 3 * rows_j), F32)
    q = iota((3 * rows_j, d_width), 0)
    q0 = jnp.where(q < rows_j, q, jnp.where(q < 2 * rows_j, q - rows_j, q - 2 * rows_j))
    low_part = (q >= rows_j) & (q < 2 * rows_j)
    d_labels, d_rank = loc_ref[0:1, :], loc_ref[8:9, :]
    pair_labels = (xb_s[:, :lanes] ^ labels[:, :lanes])[:, 0:1]
    for c in range(slab):
        kept = jnp.zeros((1, d_width), I32)
        for k in range(nirr):
            kept = jnp.where(d_labels == k, keep_ref[virt_ref[c], k], kept)
        allowed = (d_labels ^ virt_ref[c]) == pair_labels
        high, low = split(g_s[:, c, :] * jnp.where(allowed, kept.astype(F32), 0.0))
        hit_j = q0 == d_rank + c * jcap
        lhs = lhs + mm_nt(high, one(hit_j & jnp.logical_not(low_part)))
        lhs = lhs + mm_nt(low, one(hit_j & low_part))
    lhs = lhs.astype(BF16)

    def merge(t):
        xab = jnp.concatenate([al_s[tile_of(t), :]] * chunks, axis=1) ^ row_ref[...]
        for slot in range(nbuf):

            @pl.when(lax.rem(t, nbuf) == slot)
            def _():
                w_copy(t, slot).wait()

                def one_row(j, carry):
                    level = [w_s[slot][perm_ref[j, g]] for g in range(nirr)]
                    for b in range(bits):
                        odd = (xab & (1 << b)) != 0
                        level = [jnp.where(odd, level[i + 1], level[i]) for i in range(0, len(level), 2)]
                    for v in range(chunks):
                        wx_s[v, j] = level[0][:, v * 128:(v + 1) * 128]
                    return carry

                lax.fori_loop(0, rows_j, one_row, 0, unroll=4)

                @pl.when(t + nbuf < steps)
                def _():
                    w_copy(t + nbuf, slot).start()

    def contract(t):
        wx_flat = [wx_s.at[v].reshape(rows_j * tile, 128) for v in range(chunks)]
        for i in range(tile):
            high, low = split(jnp.concatenate([x[pl.ds(i, rows_j, stride=tile), :] for x in wx_flat], axis=1))
            total = mm(lhs, jnp.concatenate([high, high, low], axis=0))
            kept = jnp.where(xb_s[...] == virt_ref[row * aw + t * tile + i], total, 0.0)
            d_s[i * pairs:(i + 1) * pairs, :] = kept
        high, low = split(d_s[...])
        folded = mm_nt(high, ft_s[...]) + mm_nt(low, ft_s[...])
        for i in range(tile):
            for o in range(ncol):
                at = i * pairs + o * own
                e_s[t, spot(o), i] = folded[at:at + own]
        e_copy(t, 0).start()

    def combine(t, k):
        e_copy(t, k).wait()
        half = ncol >> (k + 1)
        stay = pl.ds(e_base(k + 1), half)
        e_s[t, stay] = e_s[t, stay] + r_s[t, pl.ds(ncol - 2 * half, half)]
        if k + 1 < hops:
            e_copy(t, k + 1).start()
        else:
            finalize(t)

    def finalize(t):
        here = tile_of(t)
        lc_s[...] = e_s[t, e_base(hops)].reshape(tile * own, lanes)
        parts = [lc_s[pl.ds(p, tile, stride=own), :] for p in range(own)]
        for off in range(nrow):
            peer = lax.rem(row + off, nrow)
            pieces = []
            for v in range(zw // lanes):
                index = idx_s[peer, here, v * lanes:(v + 1) * lanes]
                at = iota((tile, lanes), 1) + v * lanes
                piece = None
                for p in range(own):
                    if p * cap < (v + 1) * lanes and (p + 1) * cap > v * lanes:
                        moved = lanes_of(parts[p], index)
                        piece = moved if piece is None else jnp.where(at >= p * cap, moved, piece)
                pieces.append(piece)
            packed = jnp.concatenate(pieces, axis=1)
            if off == 0:
                zr_s[row, here, :] = packed
            else:
                z_s[off - 1, here, :] = packed
        for off in range(1, nrow):
            z_copy(t, off).start()
        high, low = split(jnp.concatenate(parts, axis=0))
        wide = mm(high, ft_s[...]) + mm(low, ft_s[...])
        for p in range(own):
            o_ref[p, here, :] = wide[p * tile:(p + 1) * tile]

    def in_range(t):
        return (t >= 0) & (t < steps)

    def turn(u, carry):
        pl.when(u < steps)(lambda: merge(u))
        pl.when(in_range(u - 1))(lambda: combine(u - 1, 0))
        pl.when(u < steps)(lambda: contract(u))
        for k in reversed(range(1, hops)):
            pl.when(in_range(u - 1 - lag * k))(lambda k=k: combine(u - 1 - lag * k, k))
        return carry

    lax.fori_loop(0, steps + 1 + lag * (hops - 1), turn, 0)

    def settle(t, carry):
        for off in range(1, nrow):
            z_copy(t, off).wait()
        return carry

    lax.fori_loop(0, steps, settle, 0)
    zt_s[...] = zr_s[...].reshape(nrow * aw, zw).T
    al = jnp.concatenate([al_s[...]] * chunks, axis=1)

    def finish(p, carry):
        z = zt_s[pl.ds(pl.multiple_of(p * cap, 8), cap), :]
        high = z.astype(BF16).astype(F32)
        both = jnp.concatenate([high, z - high], axis=0).astype(BF16)
        keep = (row_ref[...] ^ pair_ref[col * own + p]) == al
        o_ref[p] = jnp.where(keep, o_ref[p] - mm(pick, both), 0.0)
        return carry

    lax.fori_loop(0, own, finish, 0)


WHOLE = pl.BlockSpec(memory_space=pltpu.VMEM)
SCALARS = pl.BlockSpec(memory_space=pltpu.SMEM)


def make_plan(nrow, ncol, slab, d_width, nirr, cap, jcap, lanes, virt_irrep, label_row):
    return pl.pallas_call(
        functools.partial(plan_kernel, nrow, ncol, slab, d_width, nirr, cap, jcap, lanes),
        out_shape=(
            jax.ShapeDtypeStruct((1,), I32),
            jax.ShapeDtypeStruct((slab * jcap, lanes), I32),
            jax.ShapeDtypeStruct((16, d_width), I32),
        ),
        in_specs=[SCALARS, WHOLE],
        out_specs=(SCALARS, WHOLE, WHOLE),
        name="plan",
    )(virt_irrep, label_row)


def sparse_path(nrow, ncol, cap, jcap, lanes, amps, w, virt_irrep, pair_irrep, tile_mask, label_row, perm, loc):
    depth, aw, width = w.shape
    own_p, slab, d_width = amps.shape
    pairs = pair_irrep.shape[0]
    own = pairs // ncol
    tile = 8
    steps = aw // tile
    hops = ncol.bit_length() - 1
    nbuf = min(4, steps)
    zw = -(-own * cap // lanes) * lanes
    return pl.pallas_call(
        functools.partial(ladder_kernel, nrow, ncol, cap, jcap, nbuf, 2),
        out_shape=jax.ShapeDtypeStruct((own, aw, width), F32),
        in_specs=[SCALARS] * 4 + [WHOLE] * 3 + [pl.BlockSpec(memory_space=pl.ANY)],
        out_specs=WHOLE,
        scratch_shapes=[
            pltpu.VMEM((width // 128, slab * jcap, tile, 128), F32),
            pltpu.VMEM((pairs, slab, d_width), F32),
            pltpu.VMEM((tile * pairs, width), F32),
            pltpu.VMEM((lanes, width), BF16),
            pltpu.VMEM((steps, ncol, tile, own, lanes), F32),
            pltpu.VMEM((steps, ncol - 1, tile, own, lanes), F32),
            pltpu.VMEM((tile * own, lanes), F32),
            pltpu.VMEM((nrow - 1, aw, zw), F32),
            pltpu.VMEM((nrow, aw, zw), F32),
            pltpu.VMEM((zw, nrow * aw), F32),
            pltpu.VMEM((aw, lanes), I32),
            pltpu.VMEM((pairs, width), I32),
            pltpu.VMEM((nrow, aw, zw), I32),
            pltpu.SemaphoreType.DMA((nbuf,)),
            pltpu.SemaphoreType.DMA((nrow - 1,)),
            pltpu.SemaphoreType.DMA((nrow - 1,)),
            pltpu.SemaphoreType.DMA((steps, hops)),
            pltpu.SemaphoreType.DMA((steps, hops)),
            pltpu.SemaphoreType.DMA((steps, nrow - 1)),
            pltpu.SemaphoreType.DMA((steps, nrow - 1)),
        ] + [pltpu.VMEM((depth, tile, width), F32)] * nbuf,
        compiler_params=pltpu.CompilerParams(
            collective_id=1, has_side_effects=True, vmem_limit_bytes=60 * 1024 * 1024
        ),
        name="ladder",
    )(virt_irrep, pair_irrep, tile_mask, perm, label_row, loc, amps, w)


def mask_slab(amps, c_labels, d_labels, pair_irrep, tile_mask):
    labels_range = jnp.arange(tile_mask.shape[0], dtype=jnp.int32)
    c_onehot = (c_labels[:, None] == labels_range[None, :]).astype(F32)
    d_onehot = (d_labels[:, None] == labels_range[None, :]).astype(F32)
    by_c = jnp.sum(c_onehot[:, :, None] * tile_mask.astype(F32)[None], axis=1)
    screen = jnp.sum(by_c[:, None, :] * d_onehot[None], axis=2)
    allowed = (
        jnp.bitwise_xor(c_labels[:, None], d_labels[None, :])[None, :, :]
        == pair_irrep[:, None, None]
    )
    return amps * screen[None, :, :] * allowed.astype(F32)


def dense_path(amps, w, virt_irrep, pair_irrep, tile_mask, a_labels, d_labels, pair_labels, ncol):
    depth, aw, width = w.shape
    gathered = lax.all_gather(amps, "row", axis=0, tiled=True)
    pairs = gathered.shape[0]
    own = pairs // ncol
    masked = mask_slab(gathered, virt_irrep[:amps.shape[1]], d_labels, pair_irrep, tile_mask).reshape(pairs, depth)
    partial_sums = mm3(masked, w.reshape(depth, aw * width)).reshape(pairs, aw, width)
    owned = jnp.sum(exchange(partial_sums, "col").reshape(ncol, own, aw, width), axis=0)
    swapped = lax.all_to_all(owned, "row", split_axis=2, concat_axis=1, tiled=True)
    mirrored = owned - jnp.transpose(swapped, (0, 2, 1))
    kept = jnp.bitwise_xor(a_labels[:, None], virt_irrep[None, :])[None] == pair_labels[:, None, None]
    return mirrored * kept.astype(F32)


def local(nrow, ncol, amplitudes, integrals, virt_irrep, pair_irrep, tile_mask):
    own_p, slab, d_width = amplitudes.shape
    aw, width = integrals.shape[2:]
    depth = slab * d_width
    w = integrals.reshape(depth, aw, width)
    pairs = pair_irrep.shape[0]
    own = pairs // ncol
    nirr = tile_mask.shape[0]
    lanes = 128

    def dense(amps, whole):
        row_index = lax.axis_index("row")
        col_index = lax.axis_index("col")
        d_labels = lax.dynamic_slice_in_dim(virt_irrep, col_index * d_width, d_width)
        a_labels = lax.dynamic_slice_in_dim(virt_irrep, row_index * aw, aw)
        pair_labels = lax.dynamic_slice_in_dim(pair_irrep, col_index * own, own)
        return dense_path(amps, whole, virt_irrep, pair_irrep, tile_mask, a_labels, d_labels, pair_labels, ncol)

    if aw % 8 or own % 8 or width % lanes or ncol & (ncol - 1) or ncol < 2 or nrow < 2 or nirr != 8 or slab > 2 or aw > lanes:
        return dense(amplitudes, w)
    cap = min(-(-3 * aw // (10 * 8)) * 8, aw)
    jcap = -(-d_width // (4 * 8)) * 8
    label_row = virt_irrep[None, :]
    fits, perm, loc = make_plan(nrow, ncol, slab, d_width, nirr, cap, jcap, lanes, virt_irrep, label_row)
    return lax.cond(
        fits[0] > 0,
        lambda m, x: sparse_path(
            nrow, ncol, cap, jcap, lanes, m, x, virt_irrep, pair_irrep, tile_mask, label_row, perm, loc
        ),
        dense,
        amplitudes,
        w,
    )


def solution(mesh):
    in_specs = (P("row", None, "col"), P(None, "col", "row", None), P(), P(), P())
    out_specs = P("col", "row", None)
    body = functools.partial(local, mesh.shape["row"], mesh.shape["col"])
    return jax.shard_map(body, mesh=mesh, in_specs=in_specs, out_specs=out_specs, check_vma=False)
```

```python
import functools

import jax
import jax.numpy as jnp
from jax import lax
from jax.experimental import pallas as pl
from jax.experimental.pallas import tpu as pltpu
from jax.sharding import PartitionSpec as P

MESH = pl.DeviceIdType.MESH
F32 = jnp.float32
BF16 = jnp.bfloat16
I32 = jnp.int32


def split(x):
    high = x.astype(BF16)
    return high, (x - high.astype(F32)).astype(BF16)


def mm(a, b):
    return jnp.dot(a, b, preferred_element_type=F32)


def mm_nt(a, b):
    return lax.dot_general(a, b, (((1,), (1,)), ((), ())), preferred_element_type=F32)


def mm3(a, b):
    return jnp.dot(a, b, precision=lax.Precision.HIGHEST, preferred_element_type=F32)


def lanes_of(x, index):
    return jnp.take_along_axis(x, index, axis=1, mode="promise_in_bounds")


def exchange(blocks, axis):
    return lax.all_to_all(blocks, axis, split_axis=0, concat_axis=0, tiled=True)


def iota(shape, axis):
    return lax.broadcasted_iota(I32, shape, axis)


def one(x):
    return x.astype(F32).astype(BF16)


def plan_kernel(nrow, ncol, slab, d_width, nirr, cap, jcap, lanes, virt_ref, row_ref, fits_ref, perm_ref, loc_ref):
    width = row_ref.shape[1]
    aw = width // nrow
    col = lax.axis_index("col")
    labels = jnp.broadcast_to(row_ref[...], (nirr, width))
    onehot = one(labels == iota((nirr, width), 0))
    block, at = iota((lanes, width), 0), iota((lanes, width), 1)
    size = jnp.where(block < nrow, aw, jnp.where(block < nrow + ncol, d_width, width))
    first = jnp.where(block < nrow, block * aw, jnp.where(block < nrow + ncol, (block - nrow) * d_width, 0))
    member = (at >= first) & (at < first + size) & (block <= nrow + ncol)
    counts = mm_nt(onehot, one(member))
    lane = iota((nirr, lanes), 1)
    room = jnp.where(lane < nrow, cap, jnp.where(lane < nrow + ncol, jcap, lanes)).astype(F32)
    fits_ref[0] = 1 - jnp.max((counts > room).astype(I32))
    sel = one(iota((d_width, width), 1) == iota((d_width, width), 0) + col * d_width)
    local_labels = mm_nt(one(labels), sel).astype(I32)
    hit = (local_labels == iota((nirr, d_width), 0)).astype(F32)
    ahead = one(iota((d_width, d_width), 1) < iota((d_width, d_width), 0))
    rank = jnp.sum(hit * mm_nt(hit.astype(BF16), ahead), axis=0, keepdims=True).astype(I32)
    loc_ref[0:8, :] = jnp.broadcast_to(local_labels[0:1], (8, d_width))
    loc_ref[8:16, :] = jnp.broadcast_to(rank, (8, d_width))
    jth = one(rank == iota((jcap, d_width), 0))
    d = iota((lanes, d_width), 1)
    for c in range(slab):
        mine = (local_labels[0:1] ^ virt_ref[c]) == iota((lanes, d_width), 0)
        tens = mm_nt(jth, one(jnp.where(mine, d >> 4, 0)))
        ones = mm_nt(jth, one(jnp.where(mine, d & 15, 0)))
        perm_ref[c * jcap:(c + 1) * jcap, :] = (tens * 16.0 + ones).astype(I32) + c * d_width


def ladder_kernel(
    nrow, ncol, cap, jcap, nbuf, lag,
    virt_ref, pair_ref, keep_ref, perm_ref, row_ref, loc_ref, x_ref, w_ref,
    o_ref,
    g_s, d_s, ft_s, e_s, r_s, lc_s, z_s, zr_s, al_s, xb_s, idx_s, lhs_s, w_sem, gs_sem, gr_sem, es_sem, er_sem,
    zs_sem, zr_sem, wx_even, wx_odd, *w_s,
):
    row, col = lax.axis_index("row"), lax.axis_index("col")
    depth, aw, width = w_ref.shape
    own_p, slab, d_width = x_ref.shape
    pairs = xb_s.shape[0]
    own = pairs // ncol
    chunks, rows_j, tile, _ = wx_even.shape
    wx_s = (wx_even, wx_odd)
    steps = aw // tile
    lanes = ft_s.shape[0]
    nirr = keep_ref.shape[0]
    bits = nirr.bit_length() - 1
    hops = ncol.bit_length() - 1
    zw = idx_s.shape[2]

    def tile_of(t):
        return pl.ds(pl.multiple_of(t * tile, tile), tile)

    def w_copy(t, slot):
        return pltpu.make_async_copy(w_ref.at[:, tile_of(t), :], w_s[slot], w_sem.at[slot])

    for t in range(min(nbuf, steps)):
        w_copy(t, t).start()

    def labels_of(t):
        return jnp.concatenate([al_s[tile_of(t), :]] * chunks, axis=1) ^ row_ref[...]

    def merge_row(slot, xab, j):
        level = [w_s[slot][perm_ref[j, g]] for g in range(nirr)]
        for b in range(bits):
            odd = (xab & (1 << b)) != 0
            level = [jnp.where(odd, level[i + 1], level[i]) for i in range(0, len(level), 2)]
        for v in range(chunks):
            wx_s[slot % 2][v, j] = level[0][:, v * 128:(v + 1) * 128]

    def merge_first():
        w_copy(0, 0).wait()
        xab = labels_of(0)

        def some_rows(i, carry):
            for k in range(tile):
                merge_row(0, xab, i * tile + k)
            return carry

        lax.fori_loop(0, rows_j // tile, some_rows, 0)

        @pl.when(nbuf < steps)
        def _():
            w_copy(nbuf, 0).start()

    barrier = pltpu.get_barrier_semaphore()
    for off in range(1, nrow):
        pl.semaphore_signal(barrier, inc=1, device_id={"row": lax.rem(row + off, nrow)}, device_id_type=MESH)
    for k in range(hops):
        pl.semaphore_signal(barrier, inc=1, device_id={"col": col ^ (1 << k)}, device_id_type=MESH)

    labels = row_ref[...]

    def label_rows(i, carry):
        for k in range(tile):
            al_s[pl.ds(i * tile + k, 1), :] = jnp.full((1, lanes), virt_ref[row * aw + i * tile + k], I32)
        return carry

    lax.fori_loop(0, steps, label_rows, 0)
    pl.semaphore_wait(barrier, nrow - 1 + hops)

    mine = pl.ds(row * own_p, own_p)
    gathers = []
    for off in range(1, nrow):
        gathers.append(
            pltpu.make_async_remote_copy(
                src_ref=x_ref,
                dst_ref=g_s.at[mine],
                send_sem=gs_sem.at[off - 1],
                recv_sem=gr_sem.at[off - 1],
                device_id={"row": lax.rem(row + off, nrow)},
                device_id_type=MESH,
            )
        )
        gathers[-1].start()
    g_s[mine] = x_ref[...]

    merge_first()
    for p in range(pairs):
        xb_s[p:p + 1, :] = labels ^ pair_ref[p]

    wide_labels = jnp.broadcast_to(labels, (nirr, width))
    hit = wide_labels == iota((nirr, width), 0)
    onehot = one(hit)
    ranks = []
    for v in range(chunks):
        ahead = one(iota((lanes, width), 1) < iota((lanes, width), 0) + v * lanes)
        ranks.append(mm_nt(onehot, ahead))
    rank = jnp.sum(hit.astype(F32) * jnp.concatenate(ranks, axis=1), axis=0, keepdims=True).astype(I32)
    ft_s[...] = one(iota((lanes, width), 0) == rank)
    before = one(iota((nrow, width), 1) < iota((nrow, width), 0) * aw)
    starts = mm_nt(before, one(jnp.broadcast_to(labels, (lanes, width)) == iota((lanes, width), 0))).astype(I32)
    sel = one(iota((lanes, width), 1) == iota((lanes, width), 0) + row * aw)
    own_labels = mm_nt(one(wide_labels), sel)
    own_hit = (own_labels == iota((nirr, lanes), 0).astype(F32)).astype(F32)
    own_ahead = one(iota((lanes, lanes), 1) < iota((lanes, lanes), 0))
    own_rank = jnp.sum(own_hit * mm_nt(own_hit.astype(BF16), own_ahead), axis=0, keepdims=True).astype(I32)
    rank_of_row = jnp.broadcast_to(own_rank.astype(F32), (lanes, lanes)).T[:aw].astype(I32)
    lane = iota((1, zw), 1)
    owner, pos = jnp.zeros((1, zw), I32), lane
    for p in range(own):
        owner = jnp.where(lane >= p * cap, pair_ref[col * own + p], owner)
        pos = jnp.where(lane >= p * cap, lane - p * cap, pos)

    def places(t, carry):
        al = al_s[tile_of(t), :]
        for s in range(nrow):
            begin = jnp.broadcast_to(starts[s:s + 1], (tile, lanes))
            for v in range(zw // lanes):
                at = slice(v * lanes, (v + 1) * lanes)
                index = lanes_of(begin, al ^ owner[:, at]) + pos[:, at]
                idx_s[s, tile_of(t), at] = jnp.minimum(index, lanes - 1)
        return carry

    lax.fori_loop(0, steps, places, 0)

    def spot(owner):
        return sum(((owner >> k) & 1) << (hops - 1 - k) for k in range(hops))

    def e_base(k):
        base = 0
        for b in range(k):
            base = base + ((col >> b) & 1) * (ncol >> (b + 1))
        return base

    def e_copy(t, k):
        half = ncol >> (k + 1)
        away = e_base(k) + (1 - ((col >> k) & 1)) * half
        return pltpu.make_async_remote_copy(
            src_ref=e_s.at[t, pl.ds(away, half)],
            dst_ref=r_s.at[t, pl.ds(ncol - 2 * half, half)],
            send_sem=es_sem.at[t, k],
            recv_sem=er_sem.at[t, k],
            device_id={"col": col ^ (1 << k)},
            device_id_type=MESH,
        )

    def z_copy(t, off):
        return pltpu.make_async_remote_copy(
            src_ref=z_s.at[off - 1, tile_of(t)],
            dst_ref=zr_s.at[row, tile_of(t)],
            send_sem=zs_sem.at[off - 1],
            recv_sem=zr_sem.at[off - 1],
            device_id={"row": lax.rem(row + off, nrow)},
            device_id_type=MESH,
        )

    for copy in gathers:
        copy.wait()

    lhs = jnp.zeros((pairs, 3 * rows_j), F32)
    q = iota((3 * rows_j, d_width), 0)
    q0 = jnp.where(q < rows_j, q, jnp.where(q < 2 * rows_j, q - rows_j, q - 2 * rows_j))
    low_part = (q >= rows_j) & (q < 2 * rows_j)
    d_labels, d_rank = loc_ref[0:1, :], loc_ref[8:9, :]
    pair_labels = (xb_s[:, :lanes] ^ labels[:, :lanes])[:, 0:1]
    for c in range(slab):
        kept = jnp.zeros((1, d_width), I32)
        for k in range(nirr):
            kept = jnp.where(d_labels == k, keep_ref[virt_ref[c], k], kept)
        allowed = (d_labels ^ virt_ref[c]) == pair_labels
        high, low = split(g_s[:, c, :] * jnp.where(allowed, kept.astype(F32), 0.0))
        hit_j = q0 == d_rank + c * jcap
        lhs = lhs + mm_nt(high, one(hit_j & jnp.logical_not(low_part)))
        lhs = lhs + mm_nt(low, one(hit_j & low_part))
    lhs_s[...] = lhs.astype(BF16)

    def contract_rows(t, half, first, count):
        wx_flat = [wx_s[half].at[v].reshape(rows_j * tile, 128) for v in range(chunks)]
        rows = [jnp.concatenate([x[pl.ds(first + k, rows_j, stride=tile), :] for x in wx_flat], axis=1) for k in range(count)]
        high, low = split(jnp.concatenate(rows, axis=1))
        total = mm(lhs_s[...], jnp.concatenate([high, high, low], axis=0))
        for k in range(count):
            kept = jnp.where(
                xb_s[...] == virt_ref[row * aw + t * tile + first + k], total[:, k * width:(k + 1) * width], 0.0
            )
            d_s[(first + k) * pairs:(first + k + 1) * pairs, :] = kept

    def fold(t):
        high, low = split(d_s[...])
        folded = mm_nt(high, ft_s[...]) + mm_nt(low, ft_s[...])
        for i in range(tile):
            for o in range(ncol):
                at = i * pairs + o * own
                e_s[t, spot(o), i] = folded[at:at + own]
        e_copy(t, 0).start()

    def both(t, slot):
        w_copy(t, slot).wait()
        xab = labels_of(t)

        for i in range(0, tile, GROUP):
            contract_rows(t - 1, 1 - slot % 2, i, GROUP)
        for j in range(rows_j):
            merge_row(slot, xab, j)

        @pl.when(t + nbuf < steps)
        def _():
            w_copy(t + nbuf, slot).start()

    def combine(t, k):
        e_copy(t, k).wait()
        half = ncol >> (k + 1)
        stay = pl.ds(e_base(k + 1), half)
        e_s[t, stay] = e_s[t, stay] + r_s[t, pl.ds(ncol - 2 * half, half)]
        if k + 1 < hops:
            e_copy(t, k + 1).start()
        else:
            finalize(t)

    def finalize(t):
        here = tile_of(t)
        lc_s[...] = e_s[t, e_base(hops)].reshape(tile * own, lanes)
        parts = [lc_s[pl.ds(p, tile, stride=own), :] for p in range(own)]
        for off in range(nrow):
            peer = lax.rem(row + off, nrow)
            pieces = []
            for v in range(zw // lanes):
                index = idx_s[peer, here, v * lanes:(v + 1) * lanes]
                at = iota((tile, lanes), 1) + v * lanes
                piece = None
                for p in range(own):
                    if p * cap < (v + 1) * lanes and (p + 1) * cap > v * lanes:
                        moved = lanes_of(parts[p], index)
                        piece = moved if piece is None else jnp.where(at >= p * cap, moved, piece)
                pieces.append(piece)
            packed = jnp.concatenate(pieces, axis=1)
            if off == 0:
                zr_s[row, here, :] = packed
            else:
                z_s[off - 1, here, :] = packed
        for off in range(1, nrow):
            z_copy(t, off).start()
        high, low = split(jnp.concatenate(parts, axis=0))
        wide = mm(high, ft_s[...]) + mm(low, ft_s[...])
        for p in range(own):
            o_ref[p, here, :] = wide[p * tile:(p + 1) * tile]

    def in_range(t):
        return (t >= 0) & (t < steps)

    def turn(u, carry):
        for slot in range(nbuf):
            pl.when((u < steps) & (lax.rem(u, nbuf) == slot))(lambda slot=slot: both(u, slot))

        @pl.when(u == steps)
        def _():
            for i in range(0, tile, GROUP):
                contract_rows(steps - 1, (steps - 1) % 2, i, GROUP)

        pl.when(in_range(u - 1))(lambda: fold(u - 1))
        for k in reversed(range(hops)):
            pl.when(in_range(u - 2 - lag * k))(lambda k=k: combine(u - 2 - lag * k, k))
        return carry

    lax.fori_loop(1, steps + 2 + lag * (hops - 1), turn, 0)

    for off in range(1, nrow):
        pltpu.make_async_remote_copy(
            src_ref=z_s.at[off - 1],
            dst_ref=zr_s.at[row],
            send_sem=zs_sem.at[off - 1],
            recv_sem=zr_sem.at[off - 1],
            device_id={"row": lax.rem(row + off, nrow)},
            device_id_type=MESH,
        ).wait()
    al = jnp.concatenate([al_s[...]] * chunks, axis=1)
    for v in range(zw // lanes):
        high, low = split(zr_s[:, :, v * lanes:(v + 1) * lanes].reshape(nrow * aw, lanes))
        here = [p for p in range(own) if p * cap < (v + 1) * lanes and (p + 1) * cap > v * lanes]
        at = iota((aw, lanes), 1) + v * lanes
        pick = jnp.concatenate([one(at == rank_of_row + p * cap) for p in here], axis=0)
        wide = mm_nt(pick, high) + mm_nt(pick, low)
        for n, p in enumerate(here):
            rest = o_ref[p] - wide[n * aw:(n + 1) * aw]
            if (p + 1) * cap <= (v + 1) * lanes:
                keep = (row_ref[...] ^ pair_ref[col * own + p]) == al
                rest = jnp.where(keep, rest, 0.0)
            o_ref[p] = rest


GROUP = 2
WHOLE = pl.BlockSpec(memory_space=pltpu.VMEM)
SCALARS = pl.BlockSpec(memory_space=pltpu.SMEM)


def make_plan(nrow, ncol, slab, d_width, nirr, cap, jcap, lanes, virt_irrep, label_row):
    return pl.pallas_call(
        functools.partial(plan_kernel, nrow, ncol, slab, d_width, nirr, cap, jcap, lanes),
        out_shape=(
            jax.ShapeDtypeStruct((1,), I32),
            jax.ShapeDtypeStruct((slab * jcap, lanes), I32),
            jax.ShapeDtypeStruct((16, d_width), I32),
        ),
        in_specs=[SCALARS, WHOLE],
        out_specs=(SCALARS, WHOLE, WHOLE),
        name="plan",
    )(virt_irrep, label_row)


def sparse_path(nrow, ncol, cap, jcap, lanes, amps, w, virt_irrep, pair_irrep, tile_mask, label_row, perm, loc):
    depth, aw, width = w.shape
    own_p, slab, d_width = amps.shape
    pairs = pair_irrep.shape[0]
    own = pairs // ncol
    tile = 8
    steps = aw // tile
    hops = ncol.bit_length() - 1
    nbuf = 4
    zw = -(-own * cap // lanes) * lanes
    return pl.pallas_call(
        functools.partial(ladder_kernel, nrow, ncol, cap, jcap, nbuf, 2),
        out_shape=jax.ShapeDtypeStruct((own, aw, width), F32),
        in_specs=[SCALARS] * 4 + [WHOLE] * 3 + [pl.BlockSpec(memory_space=pl.ANY)],
        out_specs=WHOLE,
        scratch_shapes=[
            pltpu.VMEM((pairs, slab, d_width), F32),
            pltpu.VMEM((tile * pairs, width), F32),
            pltpu.VMEM((lanes, width), BF16),
            pltpu.VMEM((steps, ncol, tile, own, lanes), F32),
            pltpu.VMEM((steps, ncol - 1, tile, own, lanes), F32),
            pltpu.VMEM((tile * own, lanes), F32),
            pltpu.VMEM((nrow - 1, aw, zw), F32),
            pltpu.VMEM((nrow, aw, zw), F32),
            pltpu.VMEM((aw, lanes), I32),
            pltpu.VMEM((pairs, width), I32),
            pltpu.VMEM((nrow, aw, zw), I32),
            pltpu.VMEM((pairs, 3 * slab * jcap), BF16),
            pltpu.SemaphoreType.DMA((nbuf,)),
            pltpu.SemaphoreType.DMA((nrow - 1,)),
            pltpu.SemaphoreType.DMA((nrow - 1,)),
            pltpu.SemaphoreType.DMA((steps, hops)),
            pltpu.SemaphoreType.DMA((steps, hops)),
            pltpu.SemaphoreType.DMA((nrow - 1,)),
            pltpu.SemaphoreType.DMA((nrow - 1,)),
        ]
        + [pltpu.VMEM((width // 128, slab * jcap, tile, 128), F32)] * 2
        + [pltpu.VMEM((depth, tile, width), F32)] * nbuf,
        compiler_params=pltpu.CompilerParams(
            collective_id=1, has_side_effects=True, vmem_limit_bytes=60 * 1024 * 1024
        ),
        name="ladder",
    )(virt_irrep, pair_irrep, tile_mask, perm, label_row, loc, amps, w)


def mask_slab(amps, c_labels, d_labels, pair_irrep, tile_mask):
    labels_range = jnp.arange(tile_mask.shape[0], dtype=jnp.int32)
    c_onehot = (c_labels[:, None] == labels_range[None, :]).astype(F32)
    d_onehot = (d_labels[:, None] == labels_range[None, :]).astype(F32)
    by_c = jnp.sum(c_onehot[:, :, None] * tile_mask.astype(F32)[None], axis=1)
    screen = jnp.sum(by_c[:, None, :] * d_onehot[None], axis=2)
    allowed = (
        jnp.bitwise_xor(c_labels[:, None], d_labels[None, :])[None, :, :]
        == pair_irrep[:, None, None]
    )
    return amps * screen[None, :, :] * allowed.astype(F32)


def dense_path(amps, w, virt_irrep, pair_irrep, tile_mask, a_labels, d_labels, pair_labels, ncol):
    depth, aw, width = w.shape
    gathered = lax.all_gather(amps, "row", axis=0, tiled=True)
    pairs = gathered.shape[0]
    own = pairs // ncol
    masked = mask_slab(gathered, virt_irrep[:amps.shape[1]], d_labels, pair_irrep, tile_mask).reshape(pairs, depth)
    partial_sums = mm3(masked, w.reshape(depth, aw * width)).reshape(pairs, aw, width)
    owned = jnp.sum(exchange(partial_sums, "col").reshape(ncol, own, aw, width), axis=0)
    swapped = lax.all_to_all(owned, "row", split_axis=2, concat_axis=1, tiled=True)
    mirrored = owned - jnp.transpose(swapped, (0, 2, 1))
    kept = jnp.bitwise_xor(a_labels[:, None], virt_irrep[None, :])[None] == pair_labels[:, None, None]
    return mirrored * kept.astype(F32)


def local(nrow, ncol, amplitudes, integrals, virt_irrep, pair_irrep, tile_mask):
    own_p, slab, d_width = amplitudes.shape
    aw, width = integrals.shape[2:]
    depth = slab * d_width
    w = integrals.reshape(depth, aw, width)
    pairs = pair_irrep.shape[0]
    own = pairs // ncol
    nirr = tile_mask.shape[0]
    lanes = 128

    def dense(amps, whole):
        row_index = lax.axis_index("row")
        col_index = lax.axis_index("col")
        d_labels = lax.dynamic_slice_in_dim(virt_irrep, col_index * d_width, d_width)
        a_labels = lax.dynamic_slice_in_dim(virt_irrep, row_index * aw, aw)
        pair_labels = lax.dynamic_slice_in_dim(pair_irrep, col_index * own, own)
        return dense_path(amps, whole, virt_irrep, pair_irrep, tile_mask, a_labels, d_labels, pair_labels, ncol)

    if aw % 8 or own % 8 or width % lanes or ncol & (ncol - 1) or ncol < 2 or nrow < 2 or aw < 32 or nirr != 8 or slab > 2 or aw > lanes:
        return dense(amplitudes, w)
    cap = min(-(-3 * aw // (10 * 8)) * 8, aw)
    jcap = -(-d_width // (4 * 8)) * 8
    label_row = virt_irrep[None, :]
    fits, perm, loc = make_plan(nrow, ncol, slab, d_width, nirr, cap, jcap, lanes, virt_irrep, label_row)
    return lax.cond(
        fits[0] > 0,
        lambda m, x: sparse_path(
            nrow, ncol, cap, jcap, lanes, m, x, virt_irrep, pair_irrep, tile_mask, label_row, perm, loc
        ),
        dense,
        amplitudes,
        w,
    )


def solution(mesh):
    in_specs = (P("row", None, "col"), P(None, "col", "row", None), P(), P(), P())
    out_specs = P("col", "row", None)
    body = functools.partial(local, mesh.shape["row"], mesh.shape["col"])
    return jax.shard_map(body, mesh=mesh, in_specs=in_specs, out_specs=out_specs, check_vma=False)
```

```python
import functools

import jax
import jax.numpy as jnp
from jax import lax
from jax.experimental import pallas as pl
from jax.experimental.pallas import tpu as pltpu
from jax.sharding import PartitionSpec as P

MESH = pl.DeviceIdType.MESH
F32 = jnp.float32
BF16 = jnp.bfloat16
I32 = jnp.int32


def split(x):
    high = x.astype(BF16)
    return high, (x - high.astype(F32)).astype(BF16)


def mm(a, b):
    return jnp.dot(a, b, preferred_element_type=F32)


def mm_nt(a, b):
    return lax.dot_general(a, b, (((1,), (1,)), ((), ())), preferred_element_type=F32)


def mm3(a, b):
    return jnp.dot(a, b, precision=lax.Precision.HIGHEST, preferred_element_type=F32)


def lanes_of(x, index):
    return jnp.take_along_axis(x, index, axis=1, mode="promise_in_bounds")


def exchange(blocks, axis):
    return lax.all_to_all(blocks, axis, split_axis=0, concat_axis=0, tiled=True)


def iota(shape, axis):
    return lax.broadcasted_iota(I32, shape, axis)


def one(x):
    return x.astype(F32).astype(BF16)


def plan_kernel(nrow, ncol, slab, d_width, nirr, cap, jcap, lanes, virt_ref, flat_ref, fits_ref, perm_ref, loc_ref, row_ref):
    width = flat_ref.shape[0]
    aw = width // nrow
    col = lax.axis_index("col")
    row_ref[...] = flat_ref[...][None, :]
    labels = jnp.broadcast_to(row_ref[...], (nirr, width))
    onehot = one(labels == iota((nirr, width), 0))
    block, at = iota((lanes, width), 0), iota((lanes, width), 1)
    size = jnp.where(block < nrow, aw, jnp.where(block < nrow + ncol, d_width, width))
    first = jnp.where(block < nrow, block * aw, jnp.where(block < nrow + ncol, (block - nrow) * d_width, 0))
    member = (at >= first) & (at < first + size) & (block <= nrow + ncol)
    counts = mm_nt(onehot, one(member))
    lane = iota((nirr, lanes), 1)
    room = jnp.where(lane < nrow, cap, jnp.where(lane < nrow + ncol, jcap, lanes)).astype(F32)
    fits_ref[0] = 1 - jnp.max((counts > room).astype(I32))
    sel = one(iota((d_width, width), 1) == iota((d_width, width), 0) + col * d_width)
    local_labels = mm_nt(one(labels), sel).astype(I32)
    hit = (local_labels == iota((nirr, d_width), 0)).astype(F32)
    ahead = one(iota((d_width, d_width), 1) < iota((d_width, d_width), 0))
    rank = jnp.sum(hit * mm_nt(hit.astype(BF16), ahead), axis=0, keepdims=True).astype(I32)
    loc_ref[0:8, :] = jnp.broadcast_to(local_labels[0:1], (8, d_width))
    loc_ref[8:16, :] = jnp.broadcast_to(rank, (8, d_width))
    jth = one(rank == iota((jcap, d_width), 0))
    d = iota((lanes, d_width), 1)
    for c in range(slab):
        mine = (local_labels[0:1] ^ virt_ref[c]) == iota((lanes, d_width), 0)
        tens = mm_nt(jth, one(jnp.where(mine, d >> 4, 0)))
        ones = mm_nt(jth, one(jnp.where(mine, d & 15, 0)))
        perm_ref[c * jcap:(c + 1) * jcap, :] = (tens * 16.0 + ones).astype(I32) + c * d_width


def ladder_kernel(
    nrow, ncol, cap, jcap, nbuf, lag,
    virt_ref, pair_ref, keep_ref, perm_ref, row_ref, loc_ref, x_ref, w_ref,
    o_ref,
    g_s, d_s, ft_s, e_s, r_s, lc_s, z_s, zr_s, al_s, xb_s, idx_s, lhs_s, w_sem, gs_sem, gr_sem, es_sem, er_sem,
    zs_sem, zr_sem, wx_even, wx_odd, *w_s,
):
    row, col = lax.axis_index("row"), lax.axis_index("col")
    depth, aw, width = w_ref.shape
    own_p, slab, d_width = x_ref.shape
    pairs = xb_s.shape[0]
    own = pairs // ncol
    chunks, rows_j, tile, _ = wx_even.shape
    wx_s = (wx_even, wx_odd)
    steps = aw // tile
    lanes = ft_s.shape[0]
    nirr = keep_ref.shape[0]
    bits = nirr.bit_length() - 1
    hops = ncol.bit_length() - 1
    zw = idx_s.shape[2]

    def tile_of(t):
        return pl.ds(pl.multiple_of(t * tile, tile), tile)

    def w_copy(t, slot):
        return pltpu.make_async_copy(w_ref.at[:, tile_of(t), :], w_s[slot], w_sem.at[slot])

    for t in range(min(nbuf, steps)):
        w_copy(t, t).start()

    def labels_of(t):
        return jnp.concatenate([al_s[tile_of(t), :]] * chunks, axis=1) ^ row_ref[...]

    def merge_row(slot, xab, j):
        level = [w_s[slot][perm_ref[j, g]] for g in range(nirr)]
        for b in range(bits):
            odd = (xab & (1 << b)) != 0
            level = [jnp.where(odd, level[i + 1], level[i]) for i in range(0, len(level), 2)]
        for v in range(chunks):
            wx_s[slot % 2][v, j] = level[0][:, v * 128:(v + 1) * 128]

    def merge_first():
        w_copy(0, 0).wait()
        xab = labels_of(0)

        def some_rows(i, carry):
            for k in range(tile):
                merge_row(0, xab, i * tile + k)
            return carry

        lax.fori_loop(0, rows_j // tile, some_rows, 0)

        @pl.when(nbuf < steps)
        def _():
            w_copy(nbuf, 0).start()

    barrier = pltpu.get_barrier_semaphore()
    for off in range(1, nrow):
        pl.semaphore_signal(barrier, inc=1, device_id={"row": lax.rem(row + off, nrow)}, device_id_type=MESH)
    for k in range(hops):
        pl.semaphore_signal(barrier, inc=1, device_id={"col": col ^ (1 << k)}, device_id_type=MESH)

    labels = row_ref[...]

    def label_rows(i, carry):
        for k in range(tile):
            al_s[pl.ds(i * tile + k, 1), :] = jnp.full((1, lanes), virt_ref[row * aw + i * tile + k], I32)
        return carry

    lax.fori_loop(0, steps, label_rows, 0)
    pl.semaphore_wait(barrier, nrow - 1 + hops)

    mine = pl.ds(row * own_p, own_p)
    gathers = []
    for off in range(1, nrow):
        gathers.append(
            pltpu.make_async_remote_copy(
                src_ref=x_ref,
                dst_ref=g_s.at[mine],
                send_sem=gs_sem.at[off - 1],
                recv_sem=gr_sem.at[off - 1],
                device_id={"row": lax.rem(row + off, nrow)},
                device_id_type=MESH,
            )
        )
        gathers[-1].start()
    g_s[mine] = x_ref[...]

    merge_first()
    for p in range(pairs):
        xb_s[p:p + 1, :] = labels ^ pair_ref[p]

    wide_labels = jnp.broadcast_to(labels, (nirr, width))
    hit = wide_labels == iota((nirr, width), 0)
    onehot = one(hit)
    ranks = []
    for v in range(chunks):
        ahead = one(iota((lanes, width), 1) < iota((lanes, width), 0) + v * lanes)
        ranks.append(mm_nt(onehot, ahead))
    rank = jnp.sum(hit.astype(F32) * jnp.concatenate(ranks, axis=1), axis=0, keepdims=True).astype(I32)
    ft_s[...] = one(iota((lanes, width), 0) == rank)
    before = one(iota((nrow, width), 1) < iota((nrow, width), 0) * aw)
    starts = mm_nt(before, one(jnp.broadcast_to(labels, (lanes, width)) == iota((lanes, width), 0))).astype(I32)
    sel = one(iota((lanes, width), 1) == iota((lanes, width), 0) + row * aw)
    own_labels = mm_nt(one(wide_labels), sel)
    own_hit = (own_labels == iota((nirr, lanes), 0).astype(F32)).astype(F32)
    own_ahead = one(iota((lanes, lanes), 1) < iota((lanes, lanes), 0))
    own_rank = jnp.sum(own_hit * mm_nt(own_hit.astype(BF16), own_ahead), axis=0, keepdims=True).astype(I32)
    rank_of_row = jnp.broadcast_to(own_rank.astype(F32), (lanes, lanes)).T[:aw].astype(I32)
    lane = iota((1, zw), 1)
    owner, pos = jnp.zeros((1, zw), I32), lane
    for p in range(own):
        owner = jnp.where(lane >= p * cap, pair_ref[col * own + p], owner)
        pos = jnp.where(lane >= p * cap, lane - p * cap, pos)

    def places(t, carry):
        al = al_s[tile_of(t), :]
        for s in range(nrow):
            begin = jnp.broadcast_to(starts[s:s + 1], (tile, lanes))
            for v in range(zw // lanes):
                at = slice(v * lanes, (v + 1) * lanes)
                index = lanes_of(begin, al ^ owner[:, at]) + pos[:, at]
                idx_s[s, tile_of(t), at] = jnp.minimum(index, lanes - 1)
        return carry

    lax.fori_loop(0, steps, places, 0)

    def spot(owner):
        return sum(((owner >> k) & 1) << (hops - 1 - k) for k in range(hops))

    def e_base(k):
        base = 0
        for b in range(k):
            base = base + ((col >> b) & 1) * (ncol >> (b + 1))
        return base

    def e_copy(t, k):
        half = ncol >> (k + 1)
        away = e_base(k) + (1 - ((col >> k) & 1)) * half
        return pltpu.make_async_remote_copy(
            src_ref=e_s.at[t, pl.ds(away, half)],
            dst_ref=r_s.at[t, pl.ds(ncol - 2 * half, half)],
            send_sem=es_sem.at[t, k],
            recv_sem=er_sem.at[t, k],
            device_id={"col": col ^ (1 << k)},
            device_id_type=MESH,
        )

    def z_copy(t, off):
        return pltpu.make_async_remote_copy(
            src_ref=z_s.at[off - 1, tile_of(t)],
            dst_ref=zr_s.at[row, tile_of(t)],
            send_sem=zs_sem.at[off - 1],
            recv_sem=zr_sem.at[off - 1],
            device_id={"row": lax.rem(row + off, nrow)},
            device_id_type=MESH,
        )

    for copy in gathers:
        copy.wait()

    lhs = jnp.zeros((pairs, 3 * rows_j), F32)
    q = iota((3 * rows_j, d_width), 0)
    q0 = jnp.where(q < rows_j, q, jnp.where(q < 2 * rows_j, q - rows_j, q - 2 * rows_j))
    low_part = (q >= rows_j) & (q < 2 * rows_j)
    d_labels, d_rank = loc_ref[0:1, :], loc_ref[8:9, :]
    pair_labels = (xb_s[:, :lanes] ^ labels[:, :lanes])[:, 0:1]
    for c in range(slab):
        kept = jnp.zeros((1, d_width), I32)
        for k in range(nirr):
            kept = jnp.where(d_labels == k, keep_ref[virt_ref[c], k], kept)
        allowed = (d_labels ^ virt_ref[c]) == pair_labels
        high, low = split(g_s[:, c, :] * jnp.where(allowed, kept.astype(F32), 0.0))
        hit_j = q0 == d_rank + c * jcap
        lhs = lhs + mm_nt(high, one(hit_j & jnp.logical_not(low_part)))
        lhs = lhs + mm_nt(low, one(hit_j & low_part))
    lhs_s[...] = lhs.astype(BF16)

    def contract_rows(t, half, first, count):
        wx_flat = [wx_s[half].at[v].reshape(rows_j * tile, 128) for v in range(chunks)]
        rows = [jnp.concatenate([x[pl.ds(first + k, rows_j, stride=tile), :] for x in wx_flat], axis=1) for k in range(count)]
        high, low = split(jnp.concatenate(rows, axis=1))
        total = mm(lhs_s[...], jnp.concatenate([high, high, low], axis=0))
        for k in range(count):
            kept = jnp.where(
                xb_s[...] == virt_ref[row * aw + t * tile + first + k], total[:, k * width:(k + 1) * width], 0.0
            )
            d_s[(first + k) * pairs:(first + k + 1) * pairs, :] = kept

    def fold(t):
        high, low = split(d_s[...])
        folded = mm_nt(jnp.concatenate([high, low], axis=1), jnp.concatenate([ft_s[...]] * 2, axis=1))
        for i in range(tile):
            for o in range(ncol):
                at = i * pairs + o * own
                e_s[t, spot(o), i] = folded[at:at + own]

    def both(t, slot):
        w_copy(t, slot).wait()
        xab = labels_of(t)

        for i in range(0, tile, GROUP):
            contract_rows(t - 1, 1 - slot % 2, i, GROUP)
        fold(t - 1)
        for j in range(rows_j):
            merge_row(slot, xab, j)

        @pl.when(t + nbuf < steps)
        def _():
            w_copy(t + nbuf, slot).start()

    def combine(t, k):
        e_copy(t, k).wait()
        half = ncol >> (k + 1)
        stay = pl.ds(e_base(k + 1), half)
        e_s[t, stay] = e_s[t, stay] + r_s[t, pl.ds(ncol - 2 * half, half)]
        if k + 1 < hops:
            e_copy(t, k + 1).start()
        else:
            finalize(t)

    def finalize(t):
        here = tile_of(t)
        lc_s[...] = e_s[t, e_base(hops)].reshape(tile * own, lanes)
        parts = [lc_s[pl.ds(p, tile, stride=own), :] for p in range(own)]
        for off in range(nrow):
            peer = lax.rem(row + off, nrow)
            pieces = []
            for v in range(zw // lanes):
                index = idx_s[peer, here, v * lanes:(v + 1) * lanes]
                at = iota((tile, lanes), 1) + v * lanes
                piece = None
                for p in range(own):
                    if p * cap < (v + 1) * lanes and (p + 1) * cap > v * lanes:
                        moved = lanes_of(parts[p], index)
                        piece = moved if piece is None else jnp.where(at >= p * cap, moved, piece)
                pieces.append(piece)
            packed = jnp.concatenate(pieces, axis=1)
            if off == 0:
                zr_s[row, here, :] = packed
            else:
                z_s[off - 1, here, :] = packed
        for off in range(1, nrow):
            z_copy(t, off).start()
        high, low = split(jnp.concatenate(parts, axis=0))
        wide = mm(high, ft_s[...]) + mm(low, ft_s[...])
        for p in range(own):
            o_ref[p, here, :] = wide[p * tile:(p + 1) * tile]

    def in_range(t):
        return (t >= 0) & (t < steps)

    def turn(u, carry):
        for slot in range(nbuf):
            pl.when((u < steps) & (lax.rem(u, nbuf) == slot))(lambda slot=slot: both(u, slot))

        @pl.when(u == steps)
        def _():
            for i in range(0, tile, GROUP):
                contract_rows(steps - 1, (steps - 1) % 2, i, GROUP)
            fold(steps - 1)

        pl.when(in_range(u - 1))(lambda: e_copy(u - 1, 0).start())
        for k in range(hops):
            pl.when(in_range(u - 2 - lag * k))(lambda k=k: combine(u - 2 - lag * k, k))
        return carry

    lax.fori_loop(1, steps + 2 + lag * (hops - 1), turn, 0)

    for off in range(1, nrow):
        pltpu.make_async_remote_copy(
            src_ref=z_s.at[off - 1],
            dst_ref=zr_s.at[row],
            send_sem=zs_sem.at[off - 1],
            recv_sem=zr_sem.at[off - 1],
            device_id={"row": lax.rem(row + off, nrow)},
            device_id_type=MESH,
        ).wait()
    al = jnp.concatenate([al_s[...]] * chunks, axis=1)
    for v in range(zw // lanes):
        high, low = split(zr_s[:, :, v * lanes:(v + 1) * lanes].reshape(nrow * aw, lanes))
        here = [p for p in range(own) if p * cap < (v + 1) * lanes and (p + 1) * cap > v * lanes]
        at = iota((aw, lanes), 1) + v * lanes
        pick = jnp.concatenate([one(at == rank_of_row + p * cap) for p in here], axis=0)
        wide = mm_nt(pick, high) + mm_nt(pick, low)
        for n, p in enumerate(here):
            rest = o_ref[p] - wide[n * aw:(n + 1) * aw]
            if (p + 1) * cap <= (v + 1) * lanes:
                keep = (row_ref[...] ^ pair_ref[col * own + p]) == al
                rest = jnp.where(keep, rest, 0.0)
            o_ref[p] = rest


GROUP = 2
WHOLE = pl.BlockSpec(memory_space=pltpu.VMEM)
SCALARS = pl.BlockSpec(memory_space=pltpu.SMEM)


def make_plan(nrow, ncol, slab, d_width, nirr, cap, jcap, lanes, virt_irrep):
    return pl.pallas_call(
        functools.partial(plan_kernel, nrow, ncol, slab, d_width, nirr, cap, jcap, lanes),
        out_shape=(
            jax.ShapeDtypeStruct((1,), I32),
            jax.ShapeDtypeStruct((slab * jcap, lanes), I32),
            jax.ShapeDtypeStruct((16, d_width), I32),
            jax.ShapeDtypeStruct((1, virt_irrep.shape[0]), I32),
        ),
        in_specs=[SCALARS, WHOLE],
        out_specs=(SCALARS, WHOLE, WHOLE, WHOLE),
        name="plan",
    )(virt_irrep, virt_irrep)


def sparse_path(nrow, ncol, cap, jcap, lanes, amps, w, virt_irrep, pair_irrep, tile_mask, label_row, perm, loc):
    depth, aw, width = w.shape
    own_p, slab, d_width = amps.shape
    pairs = pair_irrep.shape[0]
    own = pairs // ncol
    tile = 8
    steps = aw // tile
    hops = ncol.bit_length() - 1
    nbuf = 4
    zw = -(-own * cap // lanes) * lanes
    return pl.pallas_call(
        functools.partial(ladder_kernel, nrow, ncol, cap, jcap, nbuf, 2),
        out_shape=jax.ShapeDtypeStruct((own, aw, width), F32),
        in_specs=[SCALARS] * 4 + [WHOLE] * 3 + [pl.BlockSpec(memory_space=pl.ANY)],
        out_specs=WHOLE,
        scratch_shapes=[
            pltpu.VMEM((pairs, slab, d_width), F32),
            pltpu.VMEM((tile * pairs, width), F32),
            pltpu.VMEM((lanes, width), BF16),
            pltpu.VMEM((steps, ncol, tile, own, lanes), F32),
            pltpu.VMEM((steps, ncol - 1, tile, own, lanes), F32),
            pltpu.VMEM((tile * own, lanes), F32),
            pltpu.VMEM((nrow - 1, aw, zw), F32),
            pltpu.VMEM((nrow, aw, zw), F32),
            pltpu.VMEM((aw, lanes), I32),
            pltpu.VMEM((pairs, width), I32),
            pltpu.VMEM((nrow, aw, zw), I32),
            pltpu.VMEM((pairs, 3 * slab * jcap), BF16),
            pltpu.SemaphoreType.DMA((nbuf,)),
            pltpu.SemaphoreType.DMA((nrow - 1,)),
            pltpu.SemaphoreType.DMA((nrow - 1,)),
            pltpu.SemaphoreType.DMA((steps, hops)),
            pltpu.SemaphoreType.DMA((steps, hops)),
            pltpu.SemaphoreType.DMA((nrow - 1,)),
            pltpu.SemaphoreType.DMA((nrow - 1,)),
        ]
        + [pltpu.VMEM((width // 128, slab * jcap, tile, 128), F32)] * 2
        + [pltpu.VMEM((depth, tile, width), F32)] * nbuf,
        compiler_params=pltpu.CompilerParams(
            collective_id=1, has_side_effects=True, vmem_limit_bytes=60 * 1024 * 1024
        ),
        name="ladder",
    )(virt_irrep, pair_irrep, tile_mask, perm, label_row, loc, amps, w)


def mask_slab(amps, c_labels, d_labels, pair_irrep, tile_mask):
    labels_range = jnp.arange(tile_mask.shape[0], dtype=jnp.int32)
    c_onehot = (c_labels[:, None] == labels_range[None, :]).astype(F32)
    d_onehot = (d_labels[:, None] == labels_range[None, :]).astype(F32)
    by_c = jnp.sum(c_onehot[:, :, None] * tile_mask.astype(F32)[None], axis=1)
    screen = jnp.sum(by_c[:, None, :] * d_onehot[None], axis=2)
    allowed = (
        jnp.bitwise_xor(c_labels[:, None], d_labels[None, :])[None, :, :]
        == pair_irrep[:, None, None]
    )
    return amps * screen[None, :, :] * allowed.astype(F32)


def dense_path(amps, w, virt_irrep, pair_irrep, tile_mask, a_labels, d_labels, pair_labels, ncol):
    depth, aw, width = w.shape
    gathered = lax.all_gather(amps, "row", axis=0, tiled=True)
    pairs = gathered.shape[0]
    own = pairs // ncol
    masked = mask_slab(gathered, virt_irrep[:amps.shape[1]], d_labels, pair_irrep, tile_mask).reshape(pairs, depth)
    partial_sums = mm3(masked, w.reshape(depth, aw * width)).reshape(pairs, aw, width)
    owned = jnp.sum(exchange(partial_sums, "col").reshape(ncol, own, aw, width), axis=0)
    swapped = lax.all_to_all(owned, "row", split_axis=2, concat_axis=1, tiled=True)
    mirrored = owned - jnp.transpose(swapped, (0, 2, 1))
    kept = jnp.bitwise_xor(a_labels[:, None], virt_irrep[None, :])[None] == pair_labels[:, None, None]
    return mirrored * kept.astype(F32)


def local(nrow, ncol, amplitudes, integrals, virt_irrep, pair_irrep, tile_mask):
    own_p, slab, d_width = amplitudes.shape
    aw, width = integrals.shape[2:]
    depth = slab * d_width
    w = integrals.reshape(depth, aw, width)
    pairs = pair_irrep.shape[0]
    own = pairs // ncol
    nirr = tile_mask.shape[0]
    lanes = 128

    def dense(amps, whole):
        row_index = lax.axis_index("row")
        col_index = lax.axis_index("col")
        d_labels = lax.dynamic_slice_in_dim(virt_irrep, col_index * d_width, d_width)
        a_labels = lax.dynamic_slice_in_dim(virt_irrep, row_index * aw, aw)
        pair_labels = lax.dynamic_slice_in_dim(pair_irrep, col_index * own, own)
        return dense_path(amps, whole, virt_irrep, pair_irrep, tile_mask, a_labels, d_labels, pair_labels, ncol)

    if aw % 8 or own % 8 or width % lanes or ncol & (ncol - 1) or ncol < 2 or nrow < 2 or aw < 32 or nirr != 8 or slab > 2 or aw > lanes:
        return dense(amplitudes, w)
    cap = min(-(-3 * aw // (10 * 8)) * 8, aw)
    jcap = -(-d_width // (4 * 8)) * 8
    fits, perm, loc, label_row = make_plan(nrow, ncol, slab, d_width, nirr, cap, jcap, lanes, virt_irrep)
    return lax.cond(
        fits[0] > 0,
        lambda m, x: sparse_path(
            nrow, ncol, cap, jcap, lanes, m, x, virt_irrep, pair_irrep, tile_mask, label_row, perm, loc
        ),
        dense,
        amplitudes,
        w,
    )


def solution(mesh):
    in_specs = (P("row", None, "col"), P(None, "col", "row", None), P(), P(), P())
    out_specs = P("col", "row", None)
    body = functools.partial(local, mesh.shape["row"], mesh.shape["col"])
    return jax.shard_map(body, mesh=mesh, in_specs=in_specs, out_specs=out_specs, check_vma=False)
```
